32 devices in a mesh: row: 8 (over y, x, core), col: 4 (over z).
Axes of the slice: x: 2, y: 2, z: 4, core: 2. Of those that a mesh axis runs over, the one named last changes fastest.
Arguments:
- corner: bfloat16 [1024, 1024], P('col'), may hold values from -6 to 6
- edge_up: bfloat16 [1024, 36, 128], P('col', None, 'row'), may hold values from -0.1875 to 0.1875
- edge_left: bfloat16 [1024, 36, 1024], P('row', None, 'col'), may hold values from -0.1875 to 0.1875
- doubled: bfloat16 [1296, 1296], replicated, may hold values from -0.15625 to 0.15625
- panel: bfloat16 [36, 1024, 512], P(None, 'col', 'row'), may hold values from -0.03125 to 0.03125
Outputs:
- corner_slab: bfloat16 [36, 36, 128, 1024], P(None, None, 'row', 'col')
- panel_product: bfloat16 [36, 128, 512], P(None, 'row', 'col')
- gram: float32 [512, 512], P('row', 'col')
The draws below stay inside these ranges and needn't reach their ends.
All inputs are finite; a program needn't handle non-finite values.
Results may differ from the reference program's by a relative error of at most 0.009.
Values may be sent and summed in bfloat16 or wider, within the bound.
A program may use at most 256 MiB of HBM per device.

```python
import jax
import jax.numpy as jnp
from jax import lax

CHI = 1024
DL = 36
SLAB_DEV = 16
ALPHA = 128
PANEL = 512
N_ROW = 8


def levels(rng, dims, shards, smallest, top_value):
    gain = 1.0
    for dim, parts in shards:
        heights = jax.random.uniform(jax.random.fold_in(jax.random.fold_in(rng, 6), dim), (parts,), jnp.float32, smallest / len(shards), top_value / len(shards))
        gain = gain * jnp.repeat(jnp.exp(heights), dims[dim] // parts).reshape((-1,) + (1,) * (len(dims) - 1 - dim))
    return gain


def bell_draw(own_key, dims, width, bound, shards=(), held_as=jnp.bfloat16):
    entries = width * jax.random.normal(own_key, dims, jnp.float32)
    if shards:
        entries = entries * levels(own_key, dims, shards, -0.22, 0.18)
    return jnp.clip(entries, -bound, bound).astype(held_as)


def setup_inputs(seed: int = 0) -> dict:
    arg_keys = jax.random.split(jax.random.key(seed), 6)
    corner = bell_draw(arg_keys[0], (CHI, CHI), 1.0, 6.0, ((0, 4),))
    edge_up = bell_draw(arg_keys[1], (CHI, DL, ALPHA), CHI ** -0.5, 0.1875, ((0, 4), (2, 8)))
    edge_left = bell_draw(arg_keys[2], (CHI, DL, CHI), CHI ** -0.5, 0.1875, ((0, 8), (2, 4)))
    doubled = bell_draw(arg_keys[3], (DL * DL, DL * DL), (DL * DL) ** -0.5, 0.15625)
    panel = bell_draw(arg_keys[4], (DL, CHI, PANEL), (CHI * DL) ** -0.5, 0.03125, ((1, 4), (2, 8)))
    return dict(corner=corner, edge_up=edge_up, edge_left=edge_left, doubled=doubled, panel=panel)


def reference(corner, edge_up, edge_left, doubled, panel):
    quad = doubled.astype(jnp.float32).reshape(DL, DL, DL, DL)
    corner_edge = lax.dot_general(edge_up.astype(jnp.float32), corner.astype(jnp.float32), (((0,), (0,)), ((), ())), precision=lax.Precision.HIGHEST, preferred_element_type=jnp.float32).astype(jnp.bfloat16)
    blocks = corner_edge.reshape(DL, N_ROW, SLAB_DEV, CHI).transpose(1, 0, 2, 3)
    left_wide = edge_left.astype(jnp.float32)
    panel_wide = panel.astype(jnp.float32)

    def one_block(block_rows):
        grown = lax.dot_general(block_rows.astype(jnp.float32), left_wide, (((2,), (0,)), ((), ())), precision=lax.Precision.HIGHEST, preferred_element_type=jnp.float32).astype(jnp.bfloat16)
        slab_block = lax.dot_general(quad, grown.astype(jnp.float32), (((0, 1), (0, 2)), ((), ())), precision=lax.Precision.HIGHEST, preferred_element_type=jnp.float32).astype(jnp.bfloat16)
        product = lax.dot_general(slab_block.astype(jnp.float32), panel_wide, (((1, 3), (0, 1)), ((), ())), precision=lax.Precision.HIGHEST, preferred_element_type=jnp.float32).astype(jnp.bfloat16)
        return slab_block, product

    slabs, products = lax.map(one_block, blocks)
    corner_slab = slabs.transpose(1, 2, 0, 3, 4).reshape(DL, DL, ALPHA, CHI)
    panel_product = products.transpose(1, 0, 2, 3).reshape(DL, ALPHA, PANEL)
    wide_product = panel_product.astype(jnp.float32)
    gram = lax.dot_general(wide_product, wide_product, (((0, 1), (0, 1)), ((), ())), precision=lax.Precision.HIGHEST, preferred_element_type=jnp.float32) / (ALPHA * DL)
    return corner_slab, panel_product, gram
```

```python
import jax
import jax.numpy as jnp
from jax import lax
from jax.experimental import pallas as pl
from jax.experimental.pallas import tpu as pltpu
from jax.sharding import PartitionSpec as P

BF = jnp.bfloat16
F32 = jnp.float32
MESH = pl.DeviceIdType.MESH
CHUNKS = 6


def remote(src, dst, send_sem, recv_sem, device):
    return pltpu.make_async_remote_copy(
        src_ref=src,
        dst_ref=dst,
        send_sem=send_sem,
        recv_sem=recv_sem,
        device_id=device,
        device_id_type=MESH,
    )


def enter(devices):
    barrier = pltpu.get_barrier_semaphore()
    for device in devices:
        pl.semaphore_signal(barrier, inc=1, device_id=device, device_id_type=MESH)
    pl.semaphore_wait(barrier, len(devices))


def grow_kernel(up, corner, left, out, every, grown, parts, sent, got, edge, sends, recvs, zs, zr, local_sem, out_sems):
    dl, delta, beta = left.shape
    dk = parts.shape[1] // 16
    step = dl // CHUNKS
    half = step // 2
    r, c = lax.axis_index("row"), lax.axis_index("col")
    core, x, y = r % 2, (r // 2) % 2, r // 4
    r_core, r_x, r_y = r + 1 - 2 * core, r + 2 - 4 * x, r + 4 - 8 * y
    r_xy = r_x + 4 - 8 * y
    to_core, to_x, to_y = (r_core, c), (r_x, c), (r_y, c)
    z = [(c + d) % 4 for d in (1, 2, 3)]
    enter([to_core, to_x, to_y] + [(r, p) for p in z])

    own = pltpu.make_async_copy(left, every.at[:, pl.ds(r * delta, delta), :], local_sem)
    own.start()

    def block(n, owner, lo, size):
        return every.at[pl.ds(n * step + lo, size), pl.ds(owner * delta, delta), :]

    def move(kind, n, owner, lo, size, device):
        ref = block(n, owner, lo, size)
        return remote(ref, ref, sends.at[kind, n], recvs.at[kind, n], device)

    def first(n):
        src = left.at[pl.ds(n * step, step)]
        dst = block(n, r, 0, step)
        for kind, device in ((0, to_x), (1, to_y), (2, to_core)):
            remote(src, dst, sends.at[kind, n], recvs.at[kind, n], device).start()

    def arrived(kind, n, owner, lo, size):
        move(kind, n, owner, lo, size, to_core).wait_recv()

    first(0)
    first(1)
    for p in range(4):
        parts[p] = jnp.dot(
            up[...], corner[:, p * 256 : (p + 1) * 256], preferred_element_type=F32
        )
        sent[p] = parts[p].astype(BF)
    z_out = [remote(sent.at[z[d]], got.at[d], zs.at[0, d], zr.at[0, d], (r, z[d])) for d in range(3)]
    for copy in z_out:
        copy.start()
    z_all = [remote(edge.at[c], edge.at[c], zs.at[1, d], zr.at[1, d], (r, z[d])) for d in range(3)]

    own.wait()

    def grow(n):
        @pl.loop(n * step, (n + 1) * step)
        def _(l):
            acc = jnp.dot(edge[0], every[l, 0:256, :], preferred_element_type=F32)
            for p in range(1, 4):
                acc += jnp.dot(
                    edge[p], every[l, p * 256 : (p + 1) * 256, :], preferred_element_type=F32
                )
            grown[:, l] = acc.astype(BF).reshape(dk, 16, beta)

        pltpu.make_async_copy(
            grown.at[:, pl.ds(n * step, step)], out.at[:, pl.ds(n * step, step)], out_sems.at[n]
        ).start()

    done = 0
    for s in range(CHUNKS + 2):
        if s + 2 < CHUNKS:
            first(s + 2)
        if s < CHUNKS:
            arrived(0, s, r_x, 0, step)
            move(4, s, r_x, half, half, to_y).start()
            move(5, s, r_x, 0, step, to_core).start()
            arrived(1, s, r_y, 0, step)
            move(3, s, r_y, 0, half, to_x).start()
            move(6, s, r_y, 0, step, to_core).start()
        if 1 <= s <= CHUNKS:
            arrived(3, s - 1, r_xy, 0, half)
            move(7, s - 1, r_xy, 0, half, to_core).start()
            arrived(4, s - 1, r_xy, half, half)
            move(8, s - 1, r_xy, half, half, to_core).start()
        if s == 2:
            for d in range(3):
                z_out[d].wait_recv()
            edge[c] = (
                parts[c] + got[0].astype(F32) + got[1].astype(F32) + got[2].astype(F32)
            ).astype(BF)
            for copy in z_all:
                copy.start()
        if s == 4:
            for copy in z_all:
                copy.wait_recv()
        if s >= 4:
            while done <= s - 2:
                for kind, lo, size in ((2, 0, step), (5, 0, step), (6, 0, step), (7, 0, half), (8, half, half)):
                    arrived(kind, done, r_core, lo, size)
                grow(done)
                done += 1
    for n in range(CHUNKS):
        for kind, size in enumerate((step, step, step, half, half, step, step, half, half)):
            move(kind, n, r, 0, size, to_core).wait_send()
        pltpu.make_async_copy(
            grown.at[:, pl.ds(n * step, step)], out.at[:, pl.ds(n * step, step)], out_sems.at[n]
        ).wait()
    for copy in z_out + z_all:
        copy.wait_send()


def grow(edge_up, corner, edge_left):
    gamma, dk, alpha = edge_up.shape
    delta, dl, beta = edge_left.shape
    rows = dk * alpha
    vmem, any_space = pl.BlockSpec(memory_space=pltpu.VMEM), pl.BlockSpec(memory_space=pl.ANY)
    dma = pltpu.SemaphoreType.DMA
    return pl.pallas_call(
        grow_kernel,
        out_shape=jax.ShapeDtypeStruct((dk, dl, alpha, beta), BF),
        in_specs=[vmem, vmem, any_space],
        out_specs=any_space,
        scratch_shapes=[
            pltpu.VMEM((dl, 8 * delta, beta), BF),
            pltpu.VMEM((dk, dl, alpha, beta), BF),
            pltpu.VMEM((4, rows, 256), F32),
            pltpu.VMEM((4, rows, 256), BF),
            pltpu.VMEM((3, rows, 256), BF),
            pltpu.VMEM((4, rows, 256), BF),
            dma((9, CHUNKS)),
            dma((9, CHUNKS)),
            dma((2, 3)),
            dma((2, 3)),
            dma,
            dma((CHUNKS,)),
        ],
        compiler_params=pltpu.CompilerParams(
            collective_id=0, has_side_effects=True, vmem_limit_bytes=52 * 2**20
        ),
        name="grow",
    )(edge_up.transpose(1, 2, 0).reshape(rows, gamma), corner, edge_left.transpose(1, 0, 2))


def finish_kernel(total_rows, partial, cols, gram, sent, got, wide, tiles, landed, zs, zr, rs, rr):
    r, c = lax.axis_index("row"), lax.axis_index("col")
    z = [(c + d) % 4 for d in (1, 2, 3)]
    others = [(r + d) % 8 for d in range(1, 8)]
    enter([(r, p) for p in z] + [(p, c) for p in others])
    for p in range(4):
        sent[p] = partial[:, p * 128 : (p + 1) * 128].astype(BF)
    out = [remote(sent.at[z[d]], got.at[d], zs.at[0, d], zr.at[0, d], (r, z[d])) for d in range(3)]
    for copy in out:
        copy.start()
    mine = partial[:, pl.ds(pl.multiple_of(c * 128, 128), 128)]
    for d in range(3):
        out[d].wait_recv()
        mine += got[d].astype(F32)
    mine = mine.astype(BF)
    wide[c] = mine
    cols[...] = mine
    back = [remote(wide.at[c], wide.at[c], zs.at[1, d], zr.at[1, d], (r, z[d])) for d in range(3)]
    for copy in back:
        copy.start()
    for copy in back:
        copy.wait_recv()
    for p in range(4):
        prod = lax.dot_general(
            wide[p], mine, (((0,), (0,)), ((), ())), preferred_element_type=F32
        ) / total_rows
        tiles[2 * p] = prod[:64].astype(BF)
        tiles[2 * p + 1] = prod[64:].astype(BF)
    spread = [
        remote(tiles.at[others[d]], landed.at[d], rs.at[d], rr.at[d], (others[d], c))
        for d in range(7)
    ]
    for copy in spread:
        copy.start()
    total = tiles[r].astype(F32)
    for d in range(7):
        spread[d].wait_recv()
        total += landed[d].astype(F32)
    gram[...] = total
    for copy in out + back + spread:
        copy.wait_send()


def finish(partial, total_rows):
    rows = partial.shape[0]
    vmem = pl.BlockSpec(memory_space=pltpu.VMEM)
    dma = pltpu.SemaphoreType.DMA

    def body(*refs):
        finish_kernel(total_rows, *refs)

    return pl.pallas_call(
        body,
        out_shape=(
            jax.ShapeDtypeStruct((rows, 128), BF),
            jax.ShapeDtypeStruct((64, 128), F32),
        ),
        in_specs=[vmem],
        out_specs=(vmem, vmem),
        scratch_shapes=[
            pltpu.VMEM((4, rows, 128), BF),
            pltpu.VMEM((3, rows, 128), BF),
            pltpu.VMEM((4, rows, 128), BF),
            pltpu.VMEM((8, 64, 128), BF),
            pltpu.VMEM((7, 64, 128), BF),
            dma((2, 3)),
            dma((2, 3)),
            dma((7,)),
            dma((7,)),
        ],
        compiler_params=pltpu.CompilerParams(
            collective_id=1, has_side_effects=True, vmem_limit_bytes=16 * 2**20
        ),
        name="finish",
    )(partial)


def general(corner, edge_up, edge_left, doubled, panel):
    dl, alpha_local = edge_up.shape[1], edge_up.shape[2]
    quad = doubled.reshape(dl, dl, dl, dl)
    partials = lax.dot_general(
        edge_up, corner, (((0,), (0,)), ((), ())), preferred_element_type=F32
    )
    corner_edge = lax.psum(partials, "col").astype(BF)
    grown = lax.dot_general(
        corner_edge,
        lax.all_gather(edge_left, "row", axis=0, tiled=True),
        (((2,), (0,)), ((), ())),
        preferred_element_type=F32,
    ).astype(BF)
    slab = lax.dot_general(
        quad, grown, (((0, 1), (0, 2)), ((), ())), preferred_element_type=F32
    ).astype(BF)
    partial_product = lax.dot_general(
        slab,
        lax.all_gather(panel, "row", axis=2, tiled=True),
        (((1, 3), (0, 1)), ((), ())),
        preferred_element_type=F32,
    )
    own_cols = lax.psum_scatter(partial_product, "col", scatter_dimension=2, tiled=True).astype(BF)
    rows_all = lax.all_gather(own_cols, "col", axis=2, tiled=True)
    total_rows = dl * alpha_local * lax.axis_size("row")
    gram = lax.psum_scatter(
        (
            lax.dot_general(
                rows_all, own_cols, (((0, 1), (0, 1)), ((), ())), preferred_element_type=F32
            )
            / total_rows
        ).astype(BF),
        "row",
        scatter_dimension=0,
        tiled=True,
    ).astype(F32)
    return (slab, own_cols, gram)


def local(corner, edge_up, edge_left, doubled, panel):
    n_row, n_col = lax.axis_size("row"), lax.axis_size("col")
    if (n_row, n_col) != (8, 4):
        return general(corner, edge_up, edge_left, doubled, panel)
    dl, alpha = edge_up.shape[1], edge_up.shape[2]
    beta = edge_left.shape[2]
    grown = grow(edge_up, corner, edge_left)
    grown, panel = lax.optimization_barrier((grown, panel))
    wide = lax.all_gather(panel, "row", axis=2, tiled=True)
    slab = (
        lax.dot_general(
            doubled,
            grown.reshape(dl * dl, alpha, beta),
            (((0,), (0,)), ((), ())),
            preferred_element_type=F32,
        )
        .astype(BF)
        .reshape(dl, dl, alpha, beta)
    )
    partial = lax.dot_general(
        slab, wide, (((1, 3), (0, 1)), ((), ())), preferred_element_type=F32
    ).reshape(dl * alpha, -1)
    cols, gram = finish(partial, dl * alpha * n_row)
    return (slab, cols.reshape(dl, alpha, -1), gram)


def solution(mesh):
    in_specs = (
        P("col", None),
        P("col", None, "row"),
        P("row", None, "col"),
        P(),
        P(None, "col", "row"),
    )
    out_specs = (P(None, None, "row", "col"), P(None, "row", "col"), P("row", "col"))
    return jax.shard_map(local, mesh=mesh, in_specs=in_specs, out_specs=out_specs, check_vma=False)
```

```python
import jax
import jax.numpy as jnp
from jax import lax
from jax.experimental import pallas as pl
from jax.experimental.pallas import tpu as pltpu
from jax.sharding import PartitionSpec as P

BF = jnp.bfloat16
F32 = jnp.float32
MESH = pl.DeviceIdType.MESH
CHUNKS = 6


def remote(src, dst, send_sem, recv_sem, device):
    return pltpu.make_async_remote_copy(
        src_ref=src,
        dst_ref=dst,
        send_sem=send_sem,
        recv_sem=recv_sem,
        device_id=device,
        device_id_type=MESH,
    )


def enter(devices):
    barrier = pltpu.get_barrier_semaphore()
    for device in devices:
        pl.semaphore_signal(barrier, inc=1, device_id=device, device_id_type=MESH)
    pl.semaphore_wait(barrier, len(devices))


def grow_kernel(up, corner, left, out, every, grown, parts, sent, got, edge, sends, recvs, zs, zr, local_sem, out_sems):
    dl, delta, beta = left.shape
    dk = parts.shape[1] // 16
    step = dl // CHUNKS
    half = step // 2
    r, c = lax.axis_index("row"), lax.axis_index("col")
    core, x, y = r % 2, (r // 2) % 2, r // 4
    r_core, r_x, r_y = r + 1 - 2 * core, r + 2 - 4 * x, r + 4 - 8 * y
    r_xy = r_x + 4 - 8 * y
    to_core, to_x, to_y = (r_core, c), (r_x, c), (r_y, c)
    z = [(c + d) % 4 for d in (1, 2, 3)]
    enter([to_core, to_x, to_y] + [(r, p) for p in z])

    own = pltpu.make_async_copy(left, every.at[:, pl.ds(r * delta, delta), :], local_sem)
    own.start()

    def block(n, owner, lo, size):
        return every.at[pl.ds(n * step + lo, size), pl.ds(owner * delta, delta), :]

    def move(kind, n, owner, lo, size, device):
        ref = block(n, owner, lo, size)
        return remote(ref, ref, sends.at[kind, n], recvs.at[kind, n], device)

    def first(n):
        src = left.at[pl.ds(n * step, step)]
        dst = block(n, r, 0, step)
        for kind, device in ((0, to_x), (1, to_y), (2, to_core)):
            remote(src, dst, sends.at[kind, n], recvs.at[kind, n], device).start()

    def arrived(kind, n, owner, lo, size):
        move(kind, n, owner, lo, size, to_core).wait_recv()

    for n in range(6):
        first(n)
    for p in range(4):
        parts[p] = jnp.dot(
            up[...], corner[:, p * 256 : (p + 1) * 256], preferred_element_type=F32
        )
        sent[p] = parts[p].astype(BF)
    z_out = [remote(sent.at[z[d]], got.at[d], zs.at[0, d], zr.at[0, d], (r, z[d])) for d in range(3)]
    for copy in z_out:
        copy.start()
    z_all = [remote(edge.at[c], edge.at[c], zs.at[1, d], zr.at[1, d], (r, z[d])) for d in range(3)]

    own.wait()

    def grow(n):
        @pl.loop(n * step, (n + 1) * step)
        def _(l):
            acc = jnp.dot(edge[0], every[l, 0:256, :], preferred_element_type=F32)
            for p in range(1, 4):
                acc += jnp.dot(
                    edge[p], every[l, p * 256 : (p + 1) * 256, :], preferred_element_type=F32
                )
            grown[:, l] = acc.astype(BF).reshape(dk, 16, beta)

        pltpu.make_async_copy(
            grown.at[:, pl.ds(n * step, step)], out.at[:, pl.ds(n * step, step)], out_sems.at[n]
        ).start()

    done = 0
    for s in range(CHUNKS + 2):
        if s + 6 < CHUNKS:
            first(s + 6)
        if s < CHUNKS:
            arrived(0, s, r_x, 0, step)
            move(4, s, r_x, half, half, to_y).start()
            move(5, s, r_x, 0, step, to_core).start()
            arrived(1, s, r_y, 0, step)
            move(3, s, r_y, 0, half, to_x).start()
            move(6, s, r_y, 0, step, to_core).start()
        if 1 <= s <= CHUNKS:
            arrived(3, s - 1, r_xy, 0, half)
            move(7, s - 1, r_xy, 0, half, to_core).start()
            arrived(4, s - 1, r_xy, half, half)
            move(8, s - 1, r_xy, half, half, to_core).start()
        if s == 2:
            for d in range(3):
                z_out[d].wait_recv()
            edge[c] = (
                parts[c] + got[0].astype(F32) + got[1].astype(F32) + got[2].astype(F32)
            ).astype(BF)
            for copy in z_all:
                copy.start()
        if s == 5:
            for copy in z_all:
                copy.wait_recv()
        if s >= 5:
            while done <= s - 2:
                for kind, lo, size in ((2, 0, step), (5, 0, step), (6, 0, step), (7, 0, half), (8, half, half)):
                    arrived(kind, done, r_core, lo, size)
                grow(done)
                done += 1
    for n in range(CHUNKS):
        for kind, size in enumerate((step, step, step, half, half, step, step, half, half)):
            move(kind, n, r, 0, size, to_core).wait_send()
        pltpu.make_async_copy(
            grown.at[:, pl.ds(n * step, step)], out.at[:, pl.ds(n * step, step)], out_sems.at[n]
        ).wait()
    for copy in z_out + z_all:
        copy.wait_send()


def grow(edge_up, corner, edge_left):
    gamma, dk, alpha = edge_up.shape
    delta, dl, beta = edge_left.shape
    rows = dk * alpha
    vmem, any_space = pl.BlockSpec(memory_space=pltpu.VMEM), pl.BlockSpec(memory_space=pl.ANY)
    dma = pltpu.SemaphoreType.DMA
    return pl.pallas_call(
        grow_kernel,
        out_shape=jax.ShapeDtypeStruct((dk, dl, alpha, beta), BF),
        in_specs=[vmem, vmem, any_space],
        out_specs=any_space,
        scratch_shapes=[
            pltpu.VMEM((dl, 8 * delta, beta), BF),
            pltpu.VMEM((dk, dl, alpha, beta), BF),
            pltpu.VMEM((4, rows, 256), F32),
            pltpu.VMEM((4, rows, 256), BF),
            pltpu.VMEM((3, rows, 256), BF),
            pltpu.VMEM((4, rows, 256), BF),
            dma((9, CHUNKS)),
            dma((9, CHUNKS)),
            dma((2, 3)),
            dma((2, 3)),
            dma,
            dma((CHUNKS,)),
        ],
        compiler_params=pltpu.CompilerParams(
            collective_id=0, has_side_effects=True, vmem_limit_bytes=52 * 2**20
        ),
        name="grow",
    )(edge_up.transpose(1, 2, 0).reshape(rows, gamma), corner, edge_left.transpose(1, 0, 2))


def finish_kernel(total_rows, partial, cols, gram, sent, got, wide, tiles, landed, zs, zr, rs, rr):
    r, c = lax.axis_index("row"), lax.axis_index("col")
    z = [(c + d) % 4 for d in (1, 2, 3)]
    others = [(r + d) % 8 for d in range(1, 8)]
    enter([(r, p) for p in z] + [(p, c) for p in others])
    for p in range(4):
        sent[p] = partial[:, p * 128 : (p + 1) * 128].astype(BF)
    out = [remote(sent.at[z[d]], got.at[d], zs.at[0, d], zr.at[0, d], (r, z[d])) for d in range(3)]
    for copy in out:
        copy.start()
    mine = partial[:, pl.ds(pl.multiple_of(c * 128, 128), 128)]
    for d in range(3):
        out[d].wait_recv()
        mine += got[d].astype(F32)
    mine = mine.astype(BF)
    wide[c] = mine
    cols[...] = mine
    back = [remote(wide.at[c], wide.at[c], zs.at[1, d], zr.at[1, d], (r, z[d])) for d in range(3)]
    for copy in back:
        copy.start()
    for copy in back:
        copy.wait_recv()
    for p in range(4):
        prod = lax.dot_general(
            wide[p], mine, (((0,), (0,)), ((), ())), preferred_element_type=F32
        ) / total_rows
        tiles[2 * p] = prod[:64].astype(BF)
        tiles[2 * p + 1] = prod[64:].astype(BF)
    spread = [
        remote(tiles.at[others[d]], landed.at[d], rs.at[d], rr.at[d], (others[d], c))
        for d in range(7)
    ]
    for copy in spread:
        copy.start()
    total = tiles[r].astype(F32)
    for d in range(7):
        spread[d].wait_recv()
        total += landed[d].astype(F32)
    gram[...] = total
    for copy in out + back + spread:
        copy.wait_send()


def finish(partial, total_rows):
    rows = partial.shape[0]
    vmem = pl.BlockSpec(memory_space=pltpu.VMEM)
    dma = pltpu.SemaphoreType.DMA

    def body(*refs):
        finish_kernel(total_rows, *refs)

    return pl.pallas_call(
        body,
        out_shape=(
            jax.ShapeDtypeStruct((rows, 128), BF),
            jax.ShapeDtypeStruct((64, 128), F32),
        ),
        in_specs=[vmem],
        out_specs=(vmem, vmem),
        scratch_shapes=[
            pltpu.VMEM((4, rows, 128), BF),
            pltpu.VMEM((3, rows, 128), BF),
            pltpu.VMEM((4, rows, 128), BF),
            pltpu.VMEM((8, 64, 128), BF),
            pltpu.VMEM((7, 64, 128), BF),
            dma((2, 3)),
            dma((2, 3)),
            dma((7,)),
            dma((7,)),
        ],
        compiler_params=pltpu.CompilerParams(
            collective_id=1, has_side_effects=True, vmem_limit_bytes=16 * 2**20
        ),
        name="finish",
    )(partial)


def general(corner, edge_up, edge_left, doubled, panel):
    dl, alpha_local = edge_up.shape[1], edge_up.shape[2]
    quad = doubled.reshape(dl, dl, dl, dl)
    partials = lax.dot_general(
        edge_up, corner, (((0,), (0,)), ((), ())), preferred_element_type=F32
    )
    corner_edge = lax.psum(partials, "col").astype(BF)
    grown = lax.dot_general(
        corner_edge,
        lax.all_gather(edge_left, "row", axis=0, tiled=True),
        (((2,), (0,)), ((), ())),
        preferred_element_type=F32,
    ).astype(BF)
    slab = lax.dot_general(
        quad, grown, (((0, 1), (0, 2)), ((), ())), preferred_element_type=F32
    ).astype(BF)
    partial_product = lax.dot_general(
        slab,
        lax.all_gather(panel, "row", axis=2, tiled=True),
        (((1, 3), (0, 1)), ((), ())),
        preferred_element_type=F32,
    )
    own_cols = lax.psum_scatter(partial_product, "col", scatter_dimension=2, tiled=True).astype(BF)
    rows_all = lax.all_gather(own_cols, "col", axis=2, tiled=True)
    total_rows = dl * alpha_local * lax.axis_size("row")
    gram = lax.psum_scatter(
        (
            lax.dot_general(
                rows_all, own_cols, (((0, 1), (0, 1)), ((), ())), preferred_element_type=F32
            )
            / total_rows
        ).astype(BF),
        "row",
        scatter_dimension=0,
        tiled=True,
    ).astype(F32)
    return (slab, own_cols, gram)


def local(corner, edge_up, edge_left, doubled, panel):
    n_row, n_col = lax.axis_size("row"), lax.axis_size("col")
    if (n_row, n_col) != (8, 4):
        return general(corner, edge_up, edge_left, doubled, panel)
    dl, alpha = edge_up.shape[1], edge_up.shape[2]
    beta = edge_left.shape[2]
    grown = grow(edge_up, corner, edge_left)
    grown, panel = lax.optimization_barrier((grown, panel))
    wide = lax.all_gather(panel, "row", axis=2, tiled=True)
    slab = (
        lax.dot_general(
            doubled,
            grown.reshape(dl * dl, alpha, beta),
            (((0,), (0,)), ((), ())),
            preferred_element_type=F32,
        )
        .astype(BF)
        .reshape(dl, dl, alpha, beta)
    )
    partial = lax.dot_general(
        slab, wide, (((1, 3), (0, 1)), ((), ())), preferred_element_type=F32
    ).reshape(dl * alpha, -1)
    cols, gram = finish(partial, dl * alpha * n_row)
    return (slab, cols.reshape(dl, alpha, -1), gram)


def solution(mesh):
    in_specs = (
        P("col", None),
        P("col", None, "row"),
        P("row", None, "col"),
        P(),
        P(None, "col", "row"),
    )
    out_specs = (P(None, None, "row", "col"), P(None, "row", "col"), P("row", "col"))
    return jax.shard_map(local, mesh=mesh, in_specs=in_specs, out_specs=out_specs, check_vma=False)
```
